32 devices in a mesh: dp: 2 (over x), pipe: 4 (over y, core), expert: 4 (over z).
Axes of the slice: x: 2, y: 2, z: 4, core: 2. Of those that a mesh axis runs over, the one named last changes fastest.
Arguments:
- tokens: bfloat16 [768, 3072], P(('dp', 'expert')), may hold values from -6 to 6
- routes: int32 [768, 2], P(('dp', 'expert')), may hold values from 0 to 3, all different within a row; in each aligned block of 96 rows (0 to 95, 96 to 191, ...) at most 50 rows name the same one
- route_weights: float32 [768, 2], P(('dp', 'expert')), may hold values from 0.2 to 1
- w_gate: bfloat16 [4, 3072, 8192], P('expert', None, 'pipe'), may hold values from -0.109375 to 0.109375
- w_up: bfloat16 [4, 3072, 8192], P('expert', None, 'pipe'), may hold values from -0.109375 to 0.109375
- w_down: bfloat16 [4, 8192, 3072], P('expert', 'pipe'), may hold values from -0.0625 to 0.0625
Outputs:
- mixed: bfloat16 [768, 3072], P(('dp', 'expert'), 'pipe')
The draws below stay inside these ranges and needn't reach their ends.
Inputs may be any that keep to these rules, and one draw needn't show every extreme that they name: `routes`: each row names two different experts. Among the 96 rows of one block no expert is named more than 50 times, a bound that some block reaches.
All inputs are finite; a program needn't handle non-finite values.
Results may differ from the reference program's by a relative error of at most 0.019.
Values may be sent and summed in bfloat16 or wider, within the bound.
No kernel may reach another device: no remote copies, remote signals or barrier semaphores. Data moves between devices by JAX's collectives and lax.ppermute only.
A program may use at most 128 MiB of HBM per device.

```python
import math
import jax
import jax.numpy as jnp
import numpy as np
from jax import lax

D = 3072
FF = 8192
TOK_DEV = 96
EXPERTS = 4
CAP = 50
FF_DEV = 2048
TOKENS = 768


def shard_levels(stream_key, shape, pieces, low, largest):
    def one(axis_at, parts):
        heights = jax.random.uniform(jax.random.fold_in(jax.random.fold_in(stream_key, 6), axis_at), (parts,), jnp.float32, low / len(pieces), largest / len(pieces))
        return jnp.repeat(jnp.exp(heights), shape[axis_at] // parts).reshape((-1,) + (1,) * (len(shape) - axis_at - 1))

    loudness = one(*pieces[0])
    for cut in pieces[1:]:
        loudness = loudness * one(*cut)
    return loudness


def deal_out(stream_key, own, number, rows, count, top, reach, skew):
    order = jax.random.permutation(stream_key, count)
    crowded, ordinary = load_shares(count, rows * top, reach, skew, True), load_shares(count, rows * top, reach, skew, False)
    places = jnp.arange(count)

    def named(tallies, offset_by):
        used = int((tallies > 0).sum())
        fixed = max(1, used // 4)
        moved = fixed + (places - fixed + offset_by * (used - fixed)) % max(1, count - fixed)
        return jnp.zeros((count,), jnp.int32).at[order[jnp.where(places < fixed, places, moved)]].set(jnp.asarray(tallies, jnp.int32))

    tallies = jnp.where(number % 4 == 0, named(crowded, number // 4), named(ordinary, number - number // 4 - 1))
    mixed = jax.random.permutation(jax.random.fold_in(own, 3), count)
    source_of, receiver = mixed[0:count // 2 * 2:2], mixed[1:count // 2 * 2:2]
    margin = jnp.minimum(tallies[source_of] - 1, reach - tallies[receiver]) // 2
    margin = jnp.where((source_of == order[0]) | (receiver == order[0]) | (tallies[receiver] == 0), 0, jnp.maximum(margin, 0))
    moved = jax.random.randint(jax.random.fold_in(own, 4), (count // 2,), 0, 1 << 20) % (margin + 1)
    tallies = tallies.at[source_of].add(-moved).at[receiver].add(moved)
    labels = jnp.searchsorted(jnp.cumsum(tallies), jnp.arange(rows * top), side="right").astype(jnp.int32)
    table = labels.reshape(top, rows).T
    table = table[jax.random.permutation(jax.random.fold_in(own, 1), rows)]
    offset_by = jax.random.randint(jax.random.fold_in(own, 2), (rows, 1), 0, top)
    return jnp.take_along_axis(table, (jnp.arange(top)[None, :] + offset_by) % top, axis=1)


def load_shares(number_of, total, most, lean, full):
    portions = [(1 << 20) // math.isqrt(grade ** lean) + 1 for grade in range(1, number_of + 1)]
    largest = most if full else min(most, max(-(-total // number_of), total * portions[0] // sum(portions)))
    least = 1 if total - largest >= number_of - 1 else 0
    counts, spare = [largest] + [least] * (number_of - 1), total - largest - least * (number_of - 1)
    while spare > 0:
        movable = [i for i in range(1, number_of) if counts[i] < largest] or [i for i in range(1, number_of) if counts[i] < most]
        whole, left = sum([portions[i] for i in movable]), spare
        for i in movable:
            more = min(most - counts[i], max(1, left * portions[i] // whole), spare)
            counts[i] = counts[i] + more
            spare = spare - more
    return np.array(counts)


def normal_values(own_key, dims, scale, reach, shards=(), kind=jnp.bfloat16):
    drawn = jax.random.normal(own_key, dims, jnp.float32) * scale
    if len(shards) > 0:
        drawn = shard_levels(own_key, dims, shards, -0.22, 0.18) * drawn
    return jnp.clip(drawn, min=-reach, max=reach).astype(kind)


def setup_inputs(seed: int = 0) -> dict:
    key_of = jax.random.split(jax.random.key(seed), 7)
    tokens = normal_values(key_of[0], (TOKENS, D), 1.0, 6.0, ((0, 8),))
    routes_keys = jax.random.split(jax.random.fold_in(key_of[1], 1), TOKENS // TOK_DEV)
    routes_turns = jax.random.permutation(jax.random.fold_in(key_of[1], 3), TOKENS // TOK_DEV)
    routes = jax.vmap(lambda own, number: deal_out(jax.random.fold_in(key_of[1], 2), own, number, TOK_DEV, EXPERTS, 2, CAP, 1))(routes_keys, routes_turns).reshape((TOKENS, 2))
    route_weights = jnp.clip(0.2 + 0.8 * jax.random.uniform(key_of[2], (TOKENS, 2), jnp.float32) ** shard_levels(key_of[2], (TOKENS, 2), ((0, 8),), -0.2, 0.2), 0.2, 1.0)
    w_gate = normal_values(key_of[3], (EXPERTS, D, FF), D ** -0.5, 0.109375, ((0, 4), (2, 4)))
    w_up = normal_values(key_of[4], (EXPERTS, D, FF), D ** -0.5, 0.109375, ((0, 4), (2, 4)))
    w_down = normal_values(key_of[5], (EXPERTS, FF, D), FF ** -0.5, 0.0625, ((0, 4), (1, 4)))
    return {"tokens": tokens, "routes": routes, "route_weights": route_weights, "w_gate": w_gate, "w_up": w_up, "w_down": w_down}


def reference(tokens, routes, route_weights, w_gate, w_up, w_down):
    blocks = TOKENS // TOK_DEV
    choices = routes.reshape(blocks, TOK_DEV * 2).astype(jnp.int32)
    expert_ids = jnp.arange(EXPERTS, dtype=jnp.int32)
    matches = (choices[:, None, :] == expert_ids[None, :, None]).astype(jnp.int32)
    rank_of = (jnp.cumsum(matches, axis=2) - 1).astype(jnp.int32)
    slot_of = jnp.sum(rank_of * matches, axis=1).astype(jnp.int32)
    doubled = jnp.repeat(tokens.reshape(blocks, TOK_DEV, D), 2, axis=1).astype(jnp.float32)
    slot_ids = jnp.arange(CAP, dtype=jnp.int32)
    hidden_blocks = FF // FF_DEV

    def one_expert(packed):
        expert_index, gate_w, up_w, down_w = packed
        picker = ((choices == expert_index)[:, None, :] & (slot_of[:, None, :] == slot_ids[None, :, None])).astype(jnp.float32)
        buffer_rows = jnp.einsum("sca,sad->scd", picker, doubled).astype(jnp.bfloat16).reshape(blocks * CAP, D)
        gate_values = jnp.dot(buffer_rows, gate_w, preferred_element_type=jnp.float32)
        up_values = jnp.dot(buffer_rows, up_w, preferred_element_type=jnp.float32)
        hidden = (jax.nn.silu(gate_values) * up_values).astype(jnp.bfloat16)
        hidden_split = hidden.reshape(blocks * CAP, hidden_blocks, FF_DEV).transpose(1, 0, 2)
        down_split = down_w.reshape(hidden_blocks, FF_DEV, D)

        def add_block(running, paired):
            hidden_piece, down_piece = paired
            block_term = jnp.dot(hidden_piece, down_piece, preferred_element_type=jnp.float32).astype(jnp.bfloat16)
            block_term = lax.optimization_barrier(block_term)
            return running + block_term.astype(jnp.float32), None

        running, _ = lax.scan(add_block, jnp.zeros((blocks * CAP, D), jnp.float32), (hidden_split, down_split))
        return running.astype(jnp.bfloat16).reshape(blocks, CAP, D)

    expert_out = lax.map(one_expert, (expert_ids, w_gate, w_up, w_down))
    block_ids = (jnp.arange(TOKENS, dtype=jnp.int32) // TOK_DEV).astype(jnp.int32)
    slot_pairs = slot_of.reshape(TOKENS, 2)
    first_out = expert_out[routes[:, 0], block_ids, slot_pairs[:, 0]].astype(jnp.float32)
    second_out = expert_out[routes[:, 1], block_ids, slot_pairs[:, 1]].astype(jnp.float32)
    mixed = route_weights[:, 0:1] * first_out + route_weights[:, 1:2] * second_out
    return mixed.astype(jnp.bfloat16)
```

```python
import functools

import jax
import jax.numpy as jnp
from jax import lax
from jax.experimental import pallas as pl
from jax.experimental.pallas import tpu as pltpu
from jax.sharding import PartitionSpec as P

F32 = jnp.float32
BF16 = jnp.bfloat16
HBM = pl.BlockSpec(memory_space=pltpu.HBM)
VMEM = pl.BlockSpec(memory_space=pltpu.VMEM)
MIB = 1 << 20


def capacity_of(tok_rows, expert_total, replica_count):
    per_expert = (2 * tok_rows + expert_total - 1) // expert_total
    return min(tok_rows, replica_count * (per_expert // replica_count + 1))


def slot_table(route_rows, expert_total):
    choices = route_rows.reshape(-1)
    expert_ids = jnp.arange(expert_total, dtype=jnp.int32)
    matches = (choices[None, :] == expert_ids[:, None]).astype(jnp.int32)
    rank_of = jnp.cumsum(matches, axis=1) - 1
    return (choices, jnp.sum(rank_of * matches, axis=0))


def on_any_mesh(tokens, routes, route_weights, w_gate, w_up, w_down):
    expert_total = w_gate.shape[0] * lax.axis_size("expert")
    pipe_count = lax.axis_size("pipe")
    hidden_width = w_gate.shape[2]
    tok_rows, model_width = tokens.shape
    capacity = capacity_of(tok_rows, expert_total, lax.axis_size("dp"))
    col_share = model_width // pipe_count
    choices, slot_of = slot_table(routes, expert_total)
    target = choices * capacity + slot_of
    column_ids = jnp.arange(expert_total * capacity, dtype=jnp.int32)
    picker = (column_ids[:, None] == target[None, :]).astype(BF16)
    own_columns = lax.dynamic_slice_in_dim(tokens, lax.axis_index("pipe") * col_share, col_share, 1)
    outgoing = jnp.dot(picker, jnp.repeat(own_columns, 2, axis=0), preferred_element_type=F32)
    outgoing = outgoing.astype(BF16).reshape(expert_total, capacity, col_share)
    arrived = lax.all_to_all(outgoing, "expert", split_axis=0, concat_axis=0, tiled=True)
    rows = lax.all_gather(arrived, "pipe", axis=2, tiled=True)
    gate_part = jnp.einsum("gsd,df->gsf", rows, w_gate[0], preferred_element_type=F32)
    up_part = jnp.einsum("gsd,df->gsf", rows, w_up[0], preferred_element_type=F32)
    hidden = (jax.nn.silu(gate_part) * up_part).astype(BF16)
    down_blocks = w_down[0].reshape(hidden_width, pipe_count, col_share)
    block_term = jnp.einsum("gsf,fke->kgse", hidden, down_blocks, preferred_element_type=F32)
    block_term = lax.optimization_barrier(block_term.astype(BF16))
    section = lax.psum_scatter(block_term, "pipe", scatter_dimension=0, tiled=True)
    summed = section.reshape(expert_total, capacity, col_share)
    returned = lax.all_to_all(summed, "expert", split_axis=0, concat_axis=0, tiled=True)
    mixing = (target[:, None] == column_ids[None, :]).astype(F32) * route_weights.reshape(-1)[:, None]
    mixing = mixing.reshape(tok_rows, 2, expert_total * capacity).sum(axis=1)
    mixed = jnp.dot(
        mixing,
        returned.reshape(expert_total * capacity, col_share).astype(F32),
        precision=lax.Precision.HIGHEST,
    )
    return mixed.astype(BF16)


def load_all(pairs, sems):
    copies = [pltpu.make_async_copy(a, b, sems.at[i]) for i, (a, b) in enumerate(pairs)]
    for copy in copies:
        copy.start()
    return copies


def wait_all(copies):
    for copy in copies:
        copy.wait()


def rows_of(w_ref, share, height):
    return w_ref.at[0, pl.ds(pl.multiple_of(share * height, height), height), :]


def cols_of(w_ref, share, width):
    return w_ref.at[0, :, pl.ds(pl.multiple_of(share * width, width), width)]


def ranks(routes_t, experts):
    tok_rows = routes_t.shape[1]
    named = (routes_t[0:1, :] == experts) | (routes_t[1:2, :] == experts)
    named = named.astype(F32)
    earlier = lax.broadcasted_iota(jnp.int32, (tok_rows, tok_rows), 0)
    later = lax.broadcasted_iota(jnp.int32, (tok_rows, tok_rows), 1)
    before = (earlier < later).astype(BF16)
    count = jnp.dot(named.astype(BF16), before, preferred_element_type=F32)
    return named, count


def expert_rows(count, expert_total):
    mine = lax.axis_index("expert")
    return jnp.bitwise_xor(lax.broadcasted_iota(jnp.int32, (count, 1), 0), mine)


def pack_kernel(pipe_count, capacity, expert_total, routes_ref, own_ref, gate_ref, *refs):
    outs, vg_ref, pick_ref, sems = refs[:expert_total], refs[-3], refs[-2], refs[-1]
    share = lax.axis_index("pipe")
    loads = load_all([(rows_of(gate_ref, share, vg_ref.shape[0]), vg_ref)], sems)
    named, count = ranks(routes_ref[...], expert_rows(max(8, expert_total), expert_total))
    padded = pick_ref.shape[0] // expert_total
    slot_ids = lax.broadcasted_iota(jnp.int32, (padded, 1), 0).astype(F32)
    for k in range(expert_total):
        chosen = (count[k : k + 1, :] == slot_ids) & (named[k : k + 1, :] > 0.5)
        pick_ref[k * padded : (k + 1) * padded, :] = chosen.astype(BF16)
    picked = jnp.dot(pick_ref[...], own_ref[...], preferred_element_type=F32).astype(BF16)
    for k in range(expert_total):
        outs[k][...] = picked[k * padded : k * padded + capacity, :]
    wait_all(loads)


def local_kernel(
    pipe_count, capacity, expert_total, routes_ref, weights_ref, tokens_ref, up_ref, gate_ref, *refs
):
    own_ref, select_ref, scale_ref, vu_ref, vg_ref, sems = refs
    tok_rows = tokens_ref.shape[0]
    height = vg_ref.shape[0]
    share = lax.axis_index("pipe")
    loads = load_all(
        [
            (rows_of(up_ref, share, height), vu_ref),
            (rows_of(gate_ref, jnp.bitwise_xor(share, 1), height), vg_ref),
        ],
        sems,
    )
    routes_t = routes_ref[...]
    experts = expert_rows(max(8, expert_total), expert_total)
    named, count = ranks(routes_t, experts)
    slot_ids = lax.broadcasted_iota(jnp.int32, (capacity, 1), 0).astype(F32)
    chosen = ((count[0:1, :] == slot_ids) & (named[0:1, :] > 0.5)).astype(BF16)
    own_ref[...] = jnp.dot(chosen, tokens_ref[...], preferred_element_type=F32).astype(BF16)
    line = lax.broadcasted_iota(jnp.int32, (tok_rows, tok_rows), 0)
    lane = lax.broadcasted_iota(jnp.int32, (tok_rows, tok_rows), 1)
    eye = line == lane
    lane_slots = lax.broadcasted_iota(jnp.int32, (1, capacity), 1).astype(F32)

    def column(row):
        return jnp.sum(jnp.where(eye, row, 0.0), axis=1, keepdims=True)

    for c in range(2):
        route = routes_t[c : c + 1, :]
        slot = jnp.sum(jnp.where(route == experts, count, 0.0), axis=0, keepdims=True)
        slot_col = column(slot)
        route_col = column(jnp.bitwise_xor(route, lax.axis_index("expert")).astype(F32))
        scale_ref[c * tok_rows : (c + 1) * tok_rows, :] = jnp.broadcast_to(
            column(weights_ref[c : c + 1, :]), (tok_rows, scale_ref.shape[1])
        )
        for k in range(expert_total):
            hit = (slot_col == lane_slots) & (route_col == float(k))
            select_ref[k, c * tok_rows : (c + 1) * tok_rows, :] = hit.astype(BF16)
    wait_all(loads)


def fetch_kernel(pipe_count, plan, gate_ref, up_ref, *refs):
    outs, sems = refs[:-1], refs[-1]
    share = lax.axis_index("pipe")
    pairs = []
    for (which, j), out in zip(plan, outs):
        source = gate_ref if which == "g" else up_ref
        pairs.append((rows_of(source, jnp.bitwise_xor(share, j), out.shape[0]), out))
    wait_all(load_all(pairs, sems))


def join_kernel(j, capacity, own_ref, *refs):
    parts, out_ref = refs[:-1], refs[-1]
    width = out_ref.shape[1]
    share = jnp.bitwise_xor(lax.axis_index("pipe"), j)
    out_ref[0:capacity, :] = own_ref[:, pl.ds(pl.multiple_of(share * width, width), width)]
    for i, part in enumerate(parts):
        out_ref[(i + 1) * capacity : (i + 2) * capacity, :] = part[...]


def gate_up_kernel(j, step, first, last, x_ref, vg_ref, vu_ref, down_ref, *refs):
    sums_in = () if first else refs[:2]
    outs = refs[len(sums_in) :]
    vd_ref, sems = outs[-2], outs[-1]
    share = jnp.bitwise_xor(lax.axis_index("pipe"), j)
    loads = load_all([(cols_of(down_ref, share, vd_ref.shape[1]), vd_ref)], sems)
    width = vg_ref.shape[1]
    for f in range(0, width, step):
        sums = []
        for i, w_ref in enumerate((vg_ref, vu_ref)):
            term = jnp.dot(x_ref[...], w_ref[:, f : f + step], preferred_element_type=F32)
            if not first:
                term += sums_in[i][:, f : f + step]
            sums.append(term)
        if last:
            gate, up = sums
            outs[0][:, f : f + step] = (gate / (1.0 + jnp.exp(-gate)) * up).astype(BF16)
        else:
            for i in range(2):
                outs[i][:, f : f + step] = sums[i]
    wait_all(loads)


def down_kernel(count, hidden_ref, *refs):
    for vd_ref, out_ref in zip(refs[:count], refs[count:]):
        term = jnp.dot(hidden_ref[...], vd_ref[...], preferred_element_type=F32)
        out_ref[...] = term.astype(out_ref.dtype)


def pair_kernel(capacity, mine_ref, other_ref, *outs):
    for k, out_ref in enumerate(outs):
        rows = slice(k * capacity, (k + 1) * capacity)
        total = mine_ref[rows, :] + other_ref[rows, :].astype(F32)
        out_ref[...] = total.astype(BF16)


def down_pair_kernel(hidden_ref, vd_ref, other_ref, out_ref):
    term = jnp.dot(hidden_ref[...], vd_ref[...], preferred_element_type=F32)
    out_ref[...] = term + other_ref[...].astype(F32)


def final_kernel(k, capacity, mine_ref, other_ref, out_ref):
    total = mine_ref[k * capacity : (k + 1) * capacity, :] + other_ref[...].astype(F32)
    out_ref[...] = total.astype(BF16)


def mix_kernel(select_ref, scale_ref, *refs):
    parts, out_ref = refs[:-1], refs[-1]
    total = None
    for k, part in enumerate(parts):
        term = jnp.dot(select_ref[k], part[...], preferred_element_type=F32)
        total = term if total is None else total + term
    tok_rows = out_ref.shape[0]
    first = total[:tok_rows, :] * scale_ref[:tok_rows, 0:1]
    second = total[tok_rows:, :] * scale_ref[tok_rows:, 0:1]
    out_ref[...] = (first + second).astype(BF16)


def call(kernel, outs, args, specs, *, scratch=(), mib, flops=0, nbytes=0, aliases=None, name):
    return pl.pallas_call(
        kernel,
        out_shape=outs,
        in_specs=specs,
        out_specs=[VMEM] * len(outs),
        scratch_shapes=scratch,
        input_output_aliases=aliases or {},
        compiler_params=pltpu.CompilerParams(vmem_limit_bytes=int(mib * MIB)),
        cost_estimate=pl.CostEstimate(flops=int(flops), bytes_accessed=int(nbytes), transcendentals=0),
        name=name,
    )(*args)


def on_device(tokens, routes, route_weights, w_gate, w_up, w_down):
    expert_total = lax.axis_size("expert")
    pipe_count = lax.axis_size("pipe")
    hidden_width = w_gate.shape[2]
    tok_rows, model_width = tokens.shape
    capacity = capacity_of(tok_rows, expert_total, lax.axis_size("dp"))
    col = model_width // pipe_count
    rows = expert_total * capacity
    piece = col * hidden_width * 2
    dma = pltpu.SemaphoreType.DMA
    others = range(1, expert_total)

    def to_core(v):
        return lax.ppermute(v, "pipe", [(i, i ^ 1) for i in range(pipe_count)])

    def to_chip(v):
        return lax.ppermute(v, "pipe", [(i, i ^ 2) for i in range(pipe_count)])

    def to_expert(v, k):
        return lax.ppermute(v, "expert", [(i, i ^ k) for i in range(expert_total)])

    def array(shape, dtype=BF16):
        return jax.ShapeDtypeStruct(shape, dtype)

    wide = pltpu.VMEM((col, hidden_width), BF16)
    tall = pltpu.VMEM((hidden_width, col), BF16)

    routes_t = routes.T
    weights_t = route_weights.T
    own = lax.dynamic_slice_in_dim(tokens, lax.axis_index("pipe") * col, col, 1)
    padded = (capacity + 15) // 16 * 16
    *packed, vg0 = call(
        functools.partial(pack_kernel, pipe_count, capacity, expert_total),
        [array((capacity, col))] * expert_total + [wide],
        (routes_t, own, w_gate),
        [VMEM, VMEM, HBM],
        scratch=[pltpu.VMEM((expert_total * padded, tok_rows), BF16), dma((1,))],
        mib=4,
        flops=2 * rows * tok_rows * col,
        nbytes=piece,
        name="pack",
    )
    order = sorted(others, reverse=True)
    arrived = {k: to_expert(packed[k], k) for k in order}

    own_rows, select, scale, vu0, vg1 = call(
        functools.partial(local_kernel, pipe_count, capacity, expert_total),
        [
            array((capacity, model_width)),
            array((expert_total, 2 * tok_rows, capacity)),
            array((2 * tok_rows, 128), F32),
            wide,
            wide,
        ],
        (routes_t, weights_t, tokens, w_up, w_gate),
        [VMEM, VMEM, VMEM, HBM, HBM],
        scratch=[dma((2,))],
        mib=4,
        flops=2 * rows * tok_rows * model_width,
        nbytes=2 * piece,
        name="local",
    )

    def fetch(plan, name):
        return call(
            functools.partial(fetch_kernel, pipe_count, plan),
            [wide] * len(plan),
            (w_gate, w_up),
            [HBM, HBM],
            scratch=[dma((len(plan),))],
            mib=1,
            nbytes=len(plan) * piece,
            name=name,
        )

    vu1, vg2 = fetch((("u", 1), ("g", 2)), "fetch_a")
    vu2, vg3 = fetch((("u", 2), ("g", 3)), "fetch_b")
    (vu3,) = fetch((("u", 3),), "fetch_c")
    vg, vu = (vg0, vg1, vg2, vg3), (vu0, vu1, vu2, vu3)

    def join(j, parts, name):
        (out,) = call(
            functools.partial(join_kernel, j, capacity),
            [array((rows, col))],
            (own_rows, *[parts[k] for k in others]),
            [VMEM] * expert_total,
            mib=2,
            nbytes=2 * rows * col,
            name=name,
        )
        return out

    crossed = {k: to_chip(arrived[k]) for k in reversed(order)}
    x0 = join(0, arrived, "join_a")
    x1 = to_core(x0)
    x2 = join(2, crossed, "join_b")
    x3 = to_core(x2)

    sums = ()
    vd = {}
    total = pltpu.VMEM((rows, hidden_width), F32)
    for j, x in enumerate((x0, x1, x2, x3)):
        first, last = j == 0, j == pipe_count - 1
        take = pipe_count - 1 - j
        outs = [pltpu.VMEM((rows, hidden_width), BF16)] if last else [total, total]
        *sums, vd[take] = call(
            functools.partial(gate_up_kernel, take, min(512, hidden_width), first, last),
            outs + [tall],
            (x, vg[j], vu[j], w_down, *sums),
            [VMEM, VMEM, VMEM, HBM] + [VMEM] * len(sums),
            scratch=[dma((1,))],
            mib=6,
            flops=4 * rows * col * hidden_width,
            nbytes=piece,
            aliases={} if first or last else {4: 0, 5: 1},
            name=f"gate_up_{j}",
        )
    (hidden,) = sums

    def down(picks, dtypes, name):
        return call(
            functools.partial(down_kernel, len(picks)),
            [array((rows, col), d) for d in dtypes],
            (hidden, *[vd[j] for j in picks]),
            [VMEM] * (1 + len(picks)),
            mib=4,
            flops=2 * rows * col * hidden_width * len(picks),
            nbytes=piece,
            name=name,
        )

    (far_other,) = down((3,), (BF16,), "down_a")
    far_in = to_core(far_other)
    far_mine, near_other = down((2, 1), (F32, BF16), "down_b")
    near_in = to_core(near_other)
    halves = call(
        functools.partial(pair_kernel, capacity),
        [array((capacity, col))] * expert_total,
        (far_mine, far_in),
        [VMEM, VMEM],
        mib=4,
        nbytes=8 * rows * col,
        name="pair",
    )
    back_order = order + [0]
    half_in = {k: to_chip(halves[k]) for k in back_order}
    (mine,) = call(
        down_pair_kernel,
        [array((rows, col), F32)],
        (hidden, vd[0], near_in),
        [VMEM] * 3,
        mib=4,
        flops=2 * rows * col * hidden_width,
        nbytes=piece,
        name="down_c",
    )
    home = {}
    for k in back_order:
        (done,) = call(
            functools.partial(final_kernel, k, capacity),
            [array((capacity, col))],
            (mine, half_in[k]),
            [VMEM, VMEM],
            mib=2,
            nbytes=8 * capacity * col,
            name=f"final_{k}",
        )
        home[k] = to_expert(done, k) if k else done
    (mixed,) = call(
        mix_kernel,
        [array((tok_rows, col))],
        (select, scale, *[home[k] for k in range(expert_total)]),
        [VMEM] * (2 + expert_total),
        mib=4,
        flops=4 * rows * tok_rows * col,
        nbytes=2 * rows * col,
        name="mix",
    )
    return mixed


def solution(mesh):
    experts = mesh.shape["expert"]

    def body(tokens, routes, route_weights, w_gate, w_up, w_down):
        col = tokens.shape[1] // mesh.shape["pipe"]
        fits = (
            mesh.shape["pipe"] == 4
            and experts & (experts - 1) == 0
            and w_gate.shape[0] == 1
            and col % 128 == 0
            and w_gate.shape[2] % 128 == 0
        )
        step = on_device if fits else on_any_mesh
        return step(tokens, routes, route_weights, w_gate, w_up, w_down)

    return jax.shard_map(
        body,
        mesh=mesh,
        in_specs=(
            P(("dp", "expert"), None),
            P(("dp", "expert"), None),
            P(("dp", "expert"), None),
            P("expert", None, "pipe"),
            P("expert", None, "pipe"),
            P("expert", "pipe", None),
        ),
        out_specs=P(("dp", "expert"), "pipe"),
        check_vma=False,
    )
```

```python
import functools

import jax
import jax.numpy as jnp
from jax import lax
from jax.experimental import pallas as pl
from jax.experimental.pallas import tpu as pltpu
from jax.sharding import PartitionSpec as P


F32 = jnp.float32
BF16 = jnp.bfloat16
HBM = pl.BlockSpec(memory_space=pltpu.HBM)
VMEM = pl.BlockSpec(memory_space=pltpu.VMEM)
MIB = 1 << 20
PACK_COST = 0
LOCAL_COST = 12 << 20


def capacity_of(tok_rows, expert_total, replica_count):
    per_expert = (2 * tok_rows + expert_total - 1) // expert_total
    return min(tok_rows, replica_count * (per_expert // replica_count + 1))


def slot_table(route_rows, expert_total):
    choices = route_rows.reshape(-1)
    expert_ids = jnp.arange(expert_total, dtype=jnp.int32)
    matches = (choices[None, :] == expert_ids[:, None]).astype(jnp.int32)
    rank_of = jnp.cumsum(matches, axis=1) - 1
    return (choices, jnp.sum(rank_of * matches, axis=0))


def on_any_mesh(tokens, routes, route_weights, w_gate, w_up, w_down):
    expert_total = w_gate.shape[0] * lax.axis_size("expert")
    pipe_count = lax.axis_size("pipe")
    hidden_width = w_gate.shape[2]
    tok_rows, model_width = tokens.shape
    capacity = capacity_of(tok_rows, expert_total, lax.axis_size("dp"))
    col_share = model_width // pipe_count
    choices, slot_of = slot_table(routes, expert_total)
    target = choices * capacity + slot_of
    column_ids = jnp.arange(expert_total * capacity, dtype=jnp.int32)
    picker = (column_ids[:, None] == target[None, :]).astype(BF16)
    own_columns = lax.dynamic_slice_in_dim(tokens, lax.axis_index("pipe") * col_share, col_share, 1)
    outgoing = jnp.dot(picker, jnp.repeat(own_columns, 2, axis=0), preferred_element_type=F32)
    outgoing = outgoing.astype(BF16).reshape(expert_total, capacity, col_share)
    arrived = lax.all_to_all(outgoing, "expert", split_axis=0, concat_axis=0, tiled=True)
    rows = lax.all_gather(arrived, "pipe", axis=2, tiled=True)
    gate_part = jnp.einsum("gsd,df->gsf", rows, w_gate[0], preferred_element_type=F32)
    up_part = jnp.einsum("gsd,df->gsf", rows, w_up[0], preferred_element_type=F32)
    hidden = (jax.nn.silu(gate_part) * up_part).astype(BF16)
    down_blocks = w_down[0].reshape(hidden_width, pipe_count, col_share)
    block_term = jnp.einsum("gsf,fke->kgse", hidden, down_blocks, preferred_element_type=F32)
    block_term = lax.optimization_barrier(block_term.astype(BF16))
    section = lax.psum_scatter(block_term, "pipe", scatter_dimension=0, tiled=True)
    summed = section.reshape(expert_total, capacity, col_share)
    returned = lax.all_to_all(summed, "expert", split_axis=0, concat_axis=0, tiled=True)
    mixing = (target[:, None] == column_ids[None, :]).astype(F32) * route_weights.reshape(-1)[:, None]
    mixing = mixing.reshape(tok_rows, 2, expert_total * capacity).sum(axis=1)
    mixed = jnp.dot(
        mixing,
        returned.reshape(expert_total * capacity, col_share).astype(F32),
        precision=lax.Precision.HIGHEST,
    )
    return mixed.astype(BF16)


def load_all(pairs, sems):
    copies = [pltpu.make_async_copy(a, b, sems.at[i]) for i, (a, b) in enumerate(pairs)]
    for copy in copies:
        copy.start()
    return copies


def wait_all(copies):
    for copy in copies:
        copy.wait()


def put_packed(out_ref, values):
    height = values.shape[0]
    for b in range(values.shape[1] // 128):
        out_ref[b * height : (b + 1) * height, :] = values[:, b * 128 : (b + 1) * 128]


def take_packed(ref, height):
    blocks = ref.shape[0] // height
    return jnp.concatenate([ref[b * height : (b + 1) * height, :] for b in range(blocks)], axis=1)


def cols_of(w_ref, share, width):
    lead = (0,) if len(w_ref.shape) == 3 else ()
    return w_ref.at[(*lead, slice(None), pl.ds(pl.multiple_of(share * width, width), width))]


def ranks(routes_t, experts):
    tok_rows = routes_t.shape[1]
    named = (routes_t[0:1, :] == experts) | (routes_t[1:2, :] == experts)
    named = named.astype(F32)
    earlier = lax.broadcasted_iota(jnp.int32, (tok_rows, tok_rows), 0)
    later = lax.broadcasted_iota(jnp.int32, (tok_rows, tok_rows), 1)
    before = (earlier < later).astype(BF16)
    count = jnp.dot(named.astype(BF16), before, preferred_element_type=F32)
    return named, count


def expert_rows(count):
    mine = lax.axis_index("expert")
    return jnp.bitwise_xor(lax.broadcasted_iota(jnp.int32, (count, 1), 0), mine)


def pack_kernel(capacity, expert_total, routes_hbm, tokens_hbm, *refs):
    outs = refs[:expert_total]
    routes_ref, own_ref, pick_ref, sems = refs[expert_total:]
    share = lax.axis_index("pipe")
    wait_all(
        load_all(
            [
                (routes_hbm, routes_ref),
                (cols_of(tokens_hbm, share, own_ref.shape[1]), own_ref),
            ],
            sems,
        )
    )
    named, count = ranks(routes_ref[...], expert_rows(max(8, expert_total)))
    padded = pick_ref.shape[0] // expert_total
    slot_ids = lax.broadcasted_iota(jnp.int32, (padded, 1), 0).astype(F32)
    for k in range(expert_total):
        chosen = (count[k : k + 1, :] == slot_ids) & (named[k : k + 1, :] > 0.5)
        pick_ref[k * padded : (k + 1) * padded, :] = chosen.astype(BF16)
    picked = jnp.dot(pick_ref[...], own_ref[...], preferred_element_type=F32).astype(BF16)
    for k in range(expert_total):
        put_packed(outs[k], picked[k * padded : k * padded + capacity, :])


def local_kernel(capacity, expert_total, routes_hbm, weights_hbm, tokens_hbm, up_ref, *refs):
    own_ref, select_ref, scale_ref, vu_ref, routes_ref, weights_ref, tokens_ref, sems = refs
    wait_all(
        load_all(
            [(routes_hbm, routes_ref), (weights_hbm, weights_ref), (tokens_hbm, tokens_ref)], sems
        )
    )
    pieces = sems.shape[0] - 3
    height = vu_ref.shape[1] // pieces
    part = [pl.ds(i * height, height) for i in range(pieces)]
    loads = load_all([(up_ref.at[0, p, :], vu_ref.at[0, p, :]) for p in part], sems.at[pl.ds(3, pieces)])

    @pl.when(lax.axis_index("pipe") >= 0)
    def _():
        local_work(
            capacity, expert_total, routes_ref, weights_ref, tokens_ref, own_ref, select_ref, scale_ref
        )

    wait_all(loads)


def local_work(
    capacity, expert_total, routes_ref, weights_ref, tokens_ref, own_ref, select_ref, scale_ref
):
    tok_rows = tokens_ref.shape[0]
    routes_t = routes_ref[...]
    experts = expert_rows(max(8, expert_total))
    named, count = ranks(routes_t, experts)
    slot_ids = lax.broadcasted_iota(jnp.int32, (capacity, 1), 0).astype(F32)
    chosen = ((count[0:1, :] == slot_ids) & (named[0:1, :] > 0.5)).astype(BF16)
    own_ref[...] = jnp.dot(chosen, tokens_ref[...], preferred_element_type=F32).astype(BF16)
    line = lax.broadcasted_iota(jnp.int32, (tok_rows, tok_rows), 0)
    lane = lax.broadcasted_iota(jnp.int32, (tok_rows, tok_rows), 1)
    eye = line == lane
    lane_slots = lax.broadcasted_iota(jnp.int32, (1, capacity), 1).astype(F32)

    def column(row):
        return jnp.sum(jnp.where(eye, row, 0.0), axis=1, keepdims=True)

    for c in range(2):
        route = routes_t[c : c + 1, :]
        slot = jnp.sum(jnp.where(route == experts, count, 0.0), axis=0, keepdims=True)
        slot_col = column(slot)
        route_col = column(jnp.bitwise_xor(route, lax.axis_index("expert")).astype(F32))
        scale_ref[c * tok_rows : (c + 1) * tok_rows, :] = jnp.broadcast_to(
            column(weights_ref[c : c + 1, :]), (tok_rows, scale_ref.shape[1])
        )
        for k in range(expert_total):
            hit = (slot_col == lane_slots) & (route_col == float(k))
            select_ref[k, c * tok_rows : (c + 1) * tok_rows, :] = hit.astype(BF16)


def join_kernel(j, capacity, own_ref, *refs):
    parts, out_ref = refs[:-1], refs[-1]
    width = out_ref.shape[1]
    share = jnp.bitwise_xor(lax.axis_index("pipe"), j)
    out_ref[0:capacity, :] = own_ref[:, pl.ds(pl.multiple_of(share * width, width), width)]
    for i, part in enumerate(parts):
        out_ref[(i + 1) * capacity : (i + 2) * capacity, :] = take_packed(part, capacity)


def gate_up_kernel(j, take, step, first, last, x_ref, vg_ref, vu_ref, down_ref, *refs):
    sums_in = () if first else refs[:2]
    outs = refs[len(sums_in) :]
    vd_ref, sems = outs[-2], outs[-1]
    index = lax.axis_index("pipe")
    loads = load_all(
        [(cols_of(down_ref, jnp.bitwise_xor(index, take), vd_ref.shape[1]), vd_ref)], sems
    )
    width, height = vg_ref.shape[-1], x_ref.shape[1]
    rows = pl.ds(pl.multiple_of(jnp.bitwise_xor(index, j) * height, height), height)

    @pl.when(index >= 0)
    def _():
        for f in range(0, width, step):
            gate = jnp.dot(x_ref[...], vg_ref[0, rows, f : f + step], preferred_element_type=F32)
            up = jnp.dot(x_ref[...], vu_ref[0, rows, f : f + step], preferred_element_type=F32)
            if not first:
                gate += sums_in[0][:, f : f + step]
                up += sums_in[1][:, f : f + step]
            if last:
                outs[0][:, f : f + step] = (gate / (1.0 + jnp.exp(-gate)) * up).astype(BF16)
            else:
                outs[0][:, f : f + step] = gate
                outs[1][:, f : f + step] = up

    wait_all(loads)


def down_kernel(count, hidden_ref, *refs):
    for vd_ref, out_ref in zip(refs[:count], refs[count:]):
        term = jnp.dot(hidden_ref[...], vd_ref[...], preferred_element_type=F32)
        out_ref[...] = term.astype(out_ref.dtype)


def pair_kernel(capacity, mine_ref, other_ref, *outs):
    for k, out_ref in enumerate(outs):
        rows = slice(k * capacity, (k + 1) * capacity)
        total = mine_ref[rows, :] + other_ref[rows, :].astype(F32)
        put_packed(out_ref, total.astype(BF16))


def down_pair_kernel(capacity, hidden_ref, vd_ref, other_ref, *outs):
    term = jnp.dot(hidden_ref[...], vd_ref[...], preferred_element_type=F32)
    total = term + other_ref[...].astype(F32)
    for k, out_ref in enumerate(outs):
        put_packed(out_ref, total[k * capacity : (k + 1) * capacity, :])


def final_kernel(mine_ref, other_ref, out_ref):
    out_ref[...] = (mine_ref[...] + other_ref[...].astype(F32)).astype(BF16)


def mix_kernel(capacity, select_ref, scale_ref, *refs):
    parts, out_ref = refs[:-1], refs[-1]
    total = None
    for k, part in enumerate(parts):
        term = jnp.dot(select_ref[k], take_packed(part, capacity), preferred_element_type=F32)
        total = term if total is None else total + term
    tok_rows = out_ref.shape[0]
    first = total[:tok_rows, :] * scale_ref[:tok_rows, 0:1]
    second = total[tok_rows:, :] * scale_ref[tok_rows:, 0:1]
    out_ref[...] = (first + second).astype(BF16)


def call(kernel, outs, args, specs, *, scratch=(), mib, flops=0, nbytes=0, aliases=None):
    return pl.pallas_call(
        kernel,
        out_shape=outs,
        in_specs=specs,
        out_specs=[VMEM] * len(outs),
        scratch_shapes=scratch,
        input_output_aliases=aliases or {},
        compiler_params=pltpu.CompilerParams(vmem_limit_bytes=int(mib * MIB)),
        cost_estimate=pl.CostEstimate(flops=int(flops), bytes_accessed=int(nbytes), transcendentals=0),
    )(*args)


def on_device(tokens, routes, route_weights, w_gate, w_up, w_down):
    expert_total = lax.axis_size("expert")
    pipe_count = lax.axis_size("pipe")
    hidden_width = w_gate.shape[2]
    tok_rows, model_width = tokens.shape
    capacity = capacity_of(tok_rows, expert_total, lax.axis_size("dp"))
    col = model_width // pipe_count
    rows = expert_total * capacity
    piece = col * hidden_width * 2
    dma = pltpu.SemaphoreType.DMA
    others = range(1, expert_total)

    def send(v, axis, shift):
        return lax.ppermute(v, axis, [(i, i ^ shift) for i in range(lax.axis_size(axis))])

    def array(shape, dtype=BF16):
        return jax.ShapeDtypeStruct(shape, dtype)

    def in_hbm(v):
        return pltpu.with_memory_space_constraint(v, pltpu.HBM)

    packed_shape = (capacity * col // 128, 128)
    tall = pltpu.VMEM((hidden_width, col), BF16)

    routes_t = routes.T
    padded = (capacity + 15) // 16 * 16
    packed = call(
        functools.partial(pack_kernel, capacity, expert_total),
        [array(packed_shape)] * expert_total,
        (in_hbm(routes_t), in_hbm(tokens)),
        [HBM, HBM],
        scratch=[
            pltpu.VMEM((2, tok_rows), jnp.int32),
            pltpu.VMEM((tok_rows, col), BF16),
            pltpu.VMEM((expert_total * padded, tok_rows), BF16),
            dma((2,)),
        ],
        mib=4,
        flops=2 * rows * tok_rows * col,
        nbytes=PACK_COST,
    )
    order = sorted(others, reverse=True)
    arrived = {k: send(packed[k], "expert", k) for k in order}

    own_rows, select, scale, vu = call(
        functools.partial(local_kernel, capacity, expert_total),
        [
            array((capacity, model_width)),
            array((expert_total, 2 * tok_rows, capacity)),
            array((2 * tok_rows, 128), F32),
            pltpu.VMEM(w_up.shape, BF16),
        ],
        (in_hbm(routes_t), in_hbm(route_weights.T), in_hbm(tokens), in_hbm(w_up)),
        [HBM, HBM, HBM, HBM],
        scratch=[
            pltpu.VMEM((2, tok_rows), jnp.int32),
            pltpu.VMEM((2, tok_rows), F32),
            pltpu.VMEM((tok_rows, model_width), BF16),
            dma((3 + pipe_count,)),
        ],
        mib=4,
        flops=2 * rows * tok_rows * model_width,
        nbytes=LOCAL_COST,
    )
    vg = pltpu.with_memory_space_constraint(w_gate, pltpu.VMEM)

    def join(j, parts):
        (out,) = call(
            functools.partial(join_kernel, j, capacity),
            [array((rows, col))],
            (own_rows, *[parts[k] for k in others]),
            [VMEM] * expert_total,
            mib=2,
            nbytes=2 * rows * col,
        )
        return out

    crossed = {k: send(arrived[k], "pipe", 2) for k in order}
    x0 = join(0, arrived)
    x1 = send(x0, "pipe", 1)
    x2 = join(2, crossed)
    x3 = send(x2, "pipe", 1)

    sums = ()
    vd = {}
    total = pltpu.VMEM((rows, hidden_width), F32)
    for j, x in enumerate((x0, x1, x2, x3)):
        first, last = j == 0, j == pipe_count - 1
        take = pipe_count - 1 - j
        outs = [pltpu.VMEM((rows, hidden_width), BF16)] if last else [total, total]
        *sums, vd[take] = call(
            functools.partial(gate_up_kernel, j, take, min(256, hidden_width), first, last),
            outs + [tall],
            (x, vg, vu, in_hbm(w_down), *sums),
            [VMEM, VMEM, VMEM, HBM] + [VMEM] * len(sums),
            scratch=[dma((1,))],
            mib=6,
            flops=4 * rows * col * hidden_width,
            nbytes=piece,
            aliases={} if first or last else {4: 0, 5: 1},
        )
    (hidden,) = sums

    def down(picks, dtypes):
        return call(
            functools.partial(down_kernel, len(picks)),
            [array((rows, col), d) for d in dtypes],
            (hidden, *[vd[j] for j in picks]),
            [VMEM] * (1 + len(picks)),
            mib=4,
            flops=2 * rows * col * hidden_width * len(picks),
            nbytes=piece,
        )

    (far_other,) = down((3,), (BF16,))
    far_in = send(far_other, "pipe", 1)
    far_mine, near_other = down((2, 1), (F32, BF16))
    near_in = send(near_other, "pipe", 1)
    halves = call(
        functools.partial(pair_kernel, capacity),
        [array(packed_shape)] * expert_total,
        (far_mine, far_in),
        [VMEM, VMEM],
        mib=4,
        nbytes=8 * rows * col,
    )
    back_order = order + [0]
    half_in = {k: send(halves[k], "pipe", 2) for k in back_order}
    mine = call(
        functools.partial(down_pair_kernel, capacity),
        [array(packed_shape, F32)] * expert_total,
        (hidden, vd[0], near_in),
        [VMEM] * 3,
        mib=4,
        flops=2 * rows * col * hidden_width,
        nbytes=piece,
    )
    home = {}
    for k in back_order:
        (done,) = call(
            final_kernel,
            [array(packed_shape)],
            (mine[k], half_in[k]),
            [VMEM, VMEM],
            mib=2,
            nbytes=8 * capacity * col,
        )
        home[k] = send(done, "expert", k) if k else done
    (mixed,) = call(
        functools.partial(mix_kernel, capacity),
        [array((tok_rows, col))],
        (select, scale, *[home[k] for k in range(expert_total)]),
        [VMEM] * (2 + expert_total),
        mib=4,
        flops=4 * rows * tok_rows * col,
        nbytes=2 * rows * col,
    )
    return mixed


def solution(mesh):
    experts = mesh.shape["expert"]

    def body(tokens, routes, route_weights, w_gate, w_up, w_down):
        col = tokens.shape[1] // mesh.shape["pipe"]
        fits = (
            mesh.shape["pipe"] == 4
            and experts & (experts - 1) == 0
            and w_gate.shape[0] == 1
            and col % 128 == 0
            and w_gate.shape[2] % 128 == 0
        )
        step = on_device if fits else on_any_mesh
        return step(tokens, routes, route_weights, w_gate, w_up, w_down)

    return jax.shard_map(
        body,
        mesh=mesh,
        in_specs=(
            P(("dp", "expert"), None),
            P(("dp", "expert"), None),
            P(("dp", "expert"), None),
            P("expert", None, "pipe"),
            P("expert", None, "pipe"),
            P("expert", "pipe", None),
        ),
        out_specs=P(("dp", "expert"), "pipe"),
        check_vma=False,
    )
```

```python
import functools

import jax
import jax.numpy as jnp
from jax import lax
from jax.experimental import pallas as pl
from jax.experimental.pallas import tpu as pltpu
from jax.sharding import PartitionSpec as P


F32 = jnp.float32
BF16 = jnp.bfloat16
HBM = pl.BlockSpec(memory_space=pltpu.HBM)
VMEM = pl.BlockSpec(memory_space=pltpu.VMEM)
MIB = 1 << 20
PACK_COST = 0
LOCAL_COST = 12 << 20


def capacity_of(tok_rows, expert_total, replica_count):
    per_expert = (2 * tok_rows + expert_total - 1) // expert_total
    return min(tok_rows, replica_count * (per_expert // replica_count + 1))


def slot_table(route_rows, expert_total):
    choices = route_rows.reshape(-1)
    expert_ids = jnp.arange(expert_total, dtype=jnp.int32)
    matches = (choices[None, :] == expert_ids[:, None]).astype(jnp.int32)
    rank_of = jnp.cumsum(matches, axis=1) - 1
    return (choices, jnp.sum(rank_of * matches, axis=0))


def on_any_mesh(tokens, routes, route_weights, w_gate, w_up, w_down):
    expert_total = w_gate.shape[0] * lax.axis_size("expert")
    pipe_count = lax.axis_size("pipe")
    hidden_width = w_gate.shape[2]
    tok_rows, model_width = tokens.shape
    capacity = capacity_of(tok_rows, expert_total, lax.axis_size("dp"))
    col_share = model_width // pipe_count
    choices, slot_of = slot_table(routes, expert_total)
    target = choices * capacity + slot_of
    column_ids = jnp.arange(expert_total * capacity, dtype=jnp.int32)
    picker = (column_ids[:, None] == target[None, :]).astype(BF16)
    own_columns = lax.dynamic_slice_in_dim(tokens, lax.axis_index("pipe") * col_share, col_share, 1)
    outgoing = jnp.dot(picker, jnp.repeat(own_columns, 2, axis=0), preferred_element_type=F32)
    outgoing = outgoing.astype(BF16).reshape(expert_total, capacity, col_share)
    arrived = lax.all_to_all(outgoing, "expert", split_axis=0, concat_axis=0, tiled=True)
    rows = lax.all_gather(arrived, "pipe", axis=2, tiled=True)
    gate_part = jnp.einsum("gsd,df->gsf", rows, w_gate[0], preferred_element_type=F32)
    up_part = jnp.einsum("gsd,df->gsf", rows, w_up[0], preferred_element_type=F32)
    hidden = (jax.nn.silu(gate_part) * up_part).astype(BF16)
    down_blocks = w_down[0].reshape(hidden_width, pipe_count, col_share)
    block_term = jnp.einsum("gsf,fke->kgse", hidden, down_blocks, preferred_element_type=F32)
    block_term = lax.optimization_barrier(block_term.astype(BF16))
    section = lax.psum_scatter(block_term, "pipe", scatter_dimension=0, tiled=True)
    summed = section.reshape(expert_total, capacity, col_share)
    returned = lax.all_to_all(summed, "expert", split_axis=0, concat_axis=0, tiled=True)
    mixing = (target[:, None] == column_ids[None, :]).astype(F32) * route_weights.reshape(-1)[:, None]
    mixing = mixing.reshape(tok_rows, 2, expert_total * capacity).sum(axis=1)
    mixed = jnp.dot(
        mixing,
        returned.reshape(expert_total * capacity, col_share).astype(F32),
        precision=lax.Precision.HIGHEST,
    )
    return mixed.astype(BF16)


def load_all(pairs, sems):
    copies = [pltpu.make_async_copy(a, b, sems.at[i]) for i, (a, b) in enumerate(pairs)]
    for copy in copies:
        copy.start()
    return copies


def wait_all(copies):
    for copy in copies:
        copy.wait()


def put_packed(out_ref, values):
    height = values.shape[0]
    for b in range(values.shape[1] // 128):
        out_ref[b * height : (b + 1) * height, :] = values[:, b * 128 : (b + 1) * 128]


def take_packed(ref, height):
    blocks = ref.shape[0] // height
    return jnp.concatenate([ref[b * height : (b + 1) * height, :] for b in range(blocks)], axis=1)


def cols_of(w_ref, share, width):
    lead = (0,) if len(w_ref.shape) == 3 else ()
    return w_ref.at[(*lead, slice(None), pl.ds(pl.multiple_of(share * width, width), width))]


def ranks(routes_t, experts):
    tok_rows = routes_t.shape[1]
    named = (routes_t[0:1, :] == experts) | (routes_t[1:2, :] == experts)
    named = named.astype(F32)
    earlier = lax.broadcasted_iota(jnp.int32, (tok_rows, tok_rows), 0)
    later = lax.broadcasted_iota(jnp.int32, (tok_rows, tok_rows), 1)
    before = (earlier < later).astype(BF16)
    count = jnp.dot(named.astype(BF16), before, preferred_element_type=F32)
    return named, count


def expert_rows(count):
    mine = lax.axis_index("expert")
    return jnp.bitwise_xor(lax.broadcasted_iota(jnp.int32, (count, 1), 0), mine)


def lead_kernel(mark_ref, *refs):
    refs[-1][...] = mark_ref[...]


def pack_kernel(capacity, expert_total, routes_hbm, tokens_hbm, *refs):
    outs = refs[: expert_total - 1]
    mark_ref, routes_ref, own_ref, pick_ref, sems = refs[expert_total - 1 :]
    share = lax.axis_index("pipe")
    routes_load, own_load = load_all(
        [(routes_hbm, routes_ref), (cols_of(tokens_hbm, share, own_ref.shape[1]), own_ref)], sems
    )
    routes_load.wait()
    named, count = ranks(routes_ref[...], expert_rows(max(8, expert_total)))
    padded = pick_ref.shape[0] // (expert_total - 1)
    slot_ids = lax.broadcasted_iota(jnp.int32, (padded, 1), 0).astype(F32)
    for k in range(1, expert_total):
        chosen = (count[k : k + 1, :] == slot_ids) & (named[k : k + 1, :] > 0.5)
        pick_ref[(k - 1) * padded : k * padded, :] = chosen.astype(BF16)
    own_load.wait()
    picked = jnp.dot(pick_ref[...], own_ref[...], preferred_element_type=F32).astype(BF16)
    for k, out_ref in enumerate(outs):
        put_packed(out_ref, picked[k * padded : k * padded + capacity, :])
    mark_ref[...] = jnp.zeros_like(mark_ref)


def local_kernel(capacity, expert_total, takes, routes_hbm, weights_hbm, tokens_hbm, down_ref, mark_ref, *refs):
    own_ref, select_ref, scale_ref, *vd_refs, routes_ref, weights_ref, tokens_ref, sems = refs
    small = load_all(
        [(routes_hbm, routes_ref), (weights_hbm, weights_ref), (tokens_hbm, tokens_ref)], sems
    )
    share = lax.axis_index("pipe")
    loads = load_all(
        [
            (cols_of(down_ref, jnp.bitwise_xor(share, take), vd_ref.shape[1]), vd_ref)
            for take, vd_ref in zip(takes, vd_refs)
        ],
        sems.at[pl.ds(len(small), len(takes))],
    )
    wait_all(small)

    @pl.when(share >= 0)
    def _():
        local_work(
            capacity, expert_total, routes_ref, weights_ref, tokens_ref, own_ref, select_ref, scale_ref
        )

    wait_all(loads)


def local_work(
    capacity, expert_total, routes_ref, weights_ref, tokens_ref, own_ref, select_ref, scale_ref
):
    tok_rows = tokens_ref.shape[0]
    routes_t = routes_ref[...]
    experts = expert_rows(max(8, expert_total))
    named, count = ranks(routes_t, experts)
    slot_ids = lax.broadcasted_iota(jnp.int32, (capacity, 1), 0).astype(F32)
    chosen = ((count[0:1, :] == slot_ids) & (named[0:1, :] > 0.5)).astype(BF16)
    own_ref[...] = jnp.dot(chosen, tokens_ref[...], preferred_element_type=F32).astype(BF16)
    line = lax.broadcasted_iota(jnp.int32, (tok_rows, tok_rows), 0)
    lane = lax.broadcasted_iota(jnp.int32, (tok_rows, tok_rows), 1)
    eye = line == lane
    lane_slots = lax.broadcasted_iota(jnp.int32, (1, capacity), 1).astype(F32)

    def column(row):
        return jnp.sum(jnp.where(eye, row, 0.0), axis=1, keepdims=True)

    for c in range(2):
        route = routes_t[c : c + 1, :]
        slot = jnp.sum(jnp.where(route == experts, count, 0.0), axis=0, keepdims=True)
        slot_col = column(slot)
        route_col = column(jnp.bitwise_xor(route, lax.axis_index("expert")).astype(F32))
        scale_ref[c * tok_rows : (c + 1) * tok_rows, :] = jnp.broadcast_to(
            column(weights_ref[c : c + 1, :]), (tok_rows, scale_ref.shape[1])
        )
        for k in range(expert_total):
            hit = (slot_col == lane_slots) & (route_col == float(k))
            select_ref[k, c * tok_rows : (c + 1) * tok_rows, :] = hit.astype(BF16)


def join_kernel(j, capacity, own_ref, *refs):
    parts, out_ref = refs[:-1], refs[-1]
    width = out_ref.shape[1]
    share = jnp.bitwise_xor(lax.axis_index("pipe"), j)
    out_ref[0:capacity, :] = own_ref[:, pl.ds(pl.multiple_of(share * width, width), width)]
    for i, part in enumerate(parts):
        out_ref[(i + 1) * capacity : (i + 2) * capacity, :] = take_packed(part, capacity)


def gate_up_kernel(j, take, step, first, last, x_ref, vg_ref, vu_ref, *refs):
    sums_in = () if first else refs[:2]
    refs = refs[len(sums_in) :]
    share = lax.axis_index("pipe")
    loads = []
    if take is not None:
        down_ref, *refs, vd_ref, sems = refs
        source = cols_of(down_ref, jnp.bitwise_xor(share, take), vd_ref.shape[1])
        loads = load_all([(source, vd_ref)], sems)
    outs = refs
    width, height = vg_ref.shape[-1], x_ref.shape[1]
    rows = pl.ds(pl.multiple_of(jnp.bitwise_xor(share, j) * height, height), height)

    @pl.when(share >= 0)
    def _():
        for f in range(0, width, step):
            gate = jnp.dot(x_ref[...], vg_ref[0, rows, f : f + step], preferred_element_type=F32)
            up = jnp.dot(x_ref[...], vu_ref[0, rows, f : f + step], preferred_element_type=F32)
            if not first:
                gate += sums_in[0][:, f : f + step]
                up += sums_in[1][:, f : f + step]
            if last:
                outs[0][:, f : f + step] = (gate / (1.0 + jnp.exp(-gate)) * up).astype(BF16)
            else:
                outs[0][:, f : f + step] = gate
                outs[1][:, f : f + step] = up

    wait_all(loads)


def down_dot(hidden_ref, vd_ref):
    return jnp.dot(hidden_ref[...], vd_ref[...], preferred_element_type=F32)


def down_kernel(count, hidden_ref, *refs):
    for vd_ref, out_ref in zip(refs[:count], refs[count:]):
        out_ref[...] = down_dot(hidden_ref, vd_ref).astype(out_ref.dtype)


def pair_kernel(capacity, mine_ref, other_ref, *outs):
    for k, out_ref in enumerate(outs):
        rows = slice(k * capacity, (k + 1) * capacity)
        total = mine_ref[rows, :] + other_ref[rows, :].astype(F32)
        put_packed(out_ref, total.astype(BF16))


def down_pair_kernel(capacity, hidden_ref, vd_ref, other_ref, *outs):
    total = down_dot(hidden_ref, vd_ref) + other_ref[...].astype(F32)
    for k, out_ref in enumerate(outs):
        put_packed(out_ref, total[k * capacity : (k + 1) * capacity, :])


def final_kernel(mine_ref, other_ref, out_ref):
    out_ref[...] = (mine_ref[...] + other_ref[...].astype(F32)).astype(BF16)


def mix_kernel(capacity, select_ref, scale_ref, *refs):
    parts, out_ref = refs[:-1], refs[-1]
    total = None
    for k, part in enumerate(parts):
        term = jnp.dot(select_ref[k], take_packed(part, capacity), preferred_element_type=F32)
        total = term if total is None else total + term
    tok_rows = out_ref.shape[0]
    first = total[:tok_rows, :] * scale_ref[:tok_rows, 0:1]
    second = total[tok_rows:, :] * scale_ref[tok_rows:, 0:1]
    out_ref[...] = (first + second).astype(BF16)


def call(kernel, outs, args, specs, *, scratch=(), mib, flops=0, nbytes=0, aliases=None):
    return pl.pallas_call(
        kernel,
        out_shape=outs,
        in_specs=specs,
        out_specs=[VMEM] * len(outs),
        scratch_shapes=scratch,
        input_output_aliases=aliases or {},
        compiler_params=pltpu.CompilerParams(vmem_limit_bytes=int(mib * MIB)),
        cost_estimate=pl.CostEstimate(flops=int(flops), bytes_accessed=int(nbytes), transcendentals=0),
    )(*args)


def on_device(tokens, routes, route_weights, w_gate, w_up, w_down):
    expert_total = lax.axis_size("expert")
    pipe_count = lax.axis_size("pipe")
    hidden_width = w_gate.shape[2]
    tok_rows, model_width = tokens.shape
    capacity = capacity_of(tok_rows, expert_total, lax.axis_size("dp"))
    col = model_width // pipe_count
    rows = expert_total * capacity
    piece = col * hidden_width * 2
    dma = pltpu.SemaphoreType.DMA
    others = range(1, expert_total)

    def send(v, axis, shift):
        return lax.ppermute(v, axis, [(i, i ^ shift) for i in range(lax.axis_size(axis))])

    def array(shape, dtype=BF16):
        return jax.ShapeDtypeStruct(shape, dtype)

    def in_hbm(v):
        return pltpu.with_memory_space_constraint(v, pltpu.HBM)

    packed_shape = (capacity * col // 128, 128)

    tall = pltpu.VMEM((hidden_width, col), BF16)
    routes_t = routes.T
    padded = (capacity + 15) // 16 * 16
    *packed, mark = call(
        functools.partial(pack_kernel, capacity, expert_total),
        [array(packed_shape)] * (expert_total - 1) + [array((8, 128), F32)],
        (in_hbm(routes_t), in_hbm(tokens)),
        [HBM, HBM],
        scratch=[
            pltpu.VMEM((2, tok_rows), jnp.int32),
            pltpu.VMEM((tok_rows, col), BF16),
            pltpu.VMEM(((expert_total - 1) * padded, tok_rows), BF16),
            dma((2,)),
        ],
        mib=4,
        flops=2 * rows * tok_rows * col,
        nbytes=PACK_COST,
    )
    (mark,) = call(
        lead_kernel,
        [array((8, 128), F32)],
        (mark, in_hbm(w_gate), in_hbm(w_up)),
        [VMEM, HBM, HBM],
        mib=1,
    )
    order = sorted(others, reverse=True)
    arrived = {k: send(packed[k - 1], "expert", k) for k in order}

    takes = (3, 2)
    own_rows, select, scale, *fetched = call(
        functools.partial(local_kernel, capacity, expert_total, takes),
        [
            array((capacity, model_width)),
            array((expert_total, 2 * tok_rows, capacity)),
            array((2 * tok_rows, 128), F32),
            *[tall for _ in takes],
        ],
        (in_hbm(routes_t), in_hbm(route_weights.T), in_hbm(tokens), in_hbm(w_down), mark),
        [HBM, HBM, HBM, HBM, VMEM],
        scratch=[
            pltpu.VMEM((2, tok_rows), jnp.int32),
            pltpu.VMEM((2, tok_rows), F32),
            pltpu.VMEM((tok_rows, model_width), BF16),
            dma((3 + len(takes),)),
        ],
        mib=4,
        flops=2 * rows * tok_rows * model_width,
        nbytes=LOCAL_COST,
    )
    vg = pltpu.with_memory_space_constraint(w_gate, pltpu.VMEM)
    vu = pltpu.with_memory_space_constraint(w_up, pltpu.VMEM)

    def join(j, parts):
        (out,) = call(
            functools.partial(join_kernel, j, capacity),
            [array((rows, col))],
            (own_rows, *[parts[k] for k in others]),
            [VMEM] * expert_total,
            mib=2,
            nbytes=2 * rows * col,
        )
        return out

    crossed = {k: send(arrived[k], "pipe", 2) for k in order}
    x0 = join(0, arrived)
    x1 = send(x0, "pipe", 1)
    x2 = join(2, crossed)
    x3 = send(x2, "pipe", 1)

    sums = ()
    vd = dict(zip(takes, fetched))
    total = pltpu.VMEM((rows, hidden_width), F32)
    for j, x in enumerate((x0, x1, x2, x3)):
        first, last = j == 0, j == pipe_count - 1
        take = {0: 1, 1: 0}.get(j)
        fetch = take is not None
        outs = call(
            functools.partial(gate_up_kernel, j, take, min(256, hidden_width), first, last),
            ([pltpu.VMEM((rows, hidden_width), BF16)] if last else [total, total]) + [tall] * fetch,
            (x, vg, vu, *sums) + (in_hbm(w_down),) * fetch,
            [VMEM] * (3 + len(sums)) + [HBM] * fetch,
            scratch=[dma((1,))] * fetch,
            mib=6,
            flops=4 * rows * col * hidden_width,
            nbytes=2 * piece,
            aliases={} if first or last else {3: 0, 4: 1},
        )
        if fetch:
            vd[take] = outs.pop() if isinstance(outs, list) else outs[-1]
        sums = tuple(outs[: 1 if last else 2])
    (hidden,) = sums

    def down(picks, dtypes):
        return call(
            functools.partial(down_kernel, len(picks)),
            [array((rows, col), d) for d in dtypes],
            (hidden, *[vd[j] for j in picks]),
            [VMEM] * (1 + len(picks)),
            mib=4,
            flops=2 * rows * col * hidden_width * len(picks),
            nbytes=piece,
        )

    (far_other,) = down((3,), (BF16,))
    far_in = send(far_other, "pipe", 1)
    far_mine, near_other = down((2, 1), (F32, BF16))
    near_in = send(near_other, "pipe", 1)
    halves = call(
        functools.partial(pair_kernel, capacity),
        [array(packed_shape)] * expert_total,
        (far_mine, far_in),
        [VMEM, VMEM],
        mib=4,
        nbytes=8 * rows * col,
    )
    back_order = back_order_of(expert_total)
    half_in = {k: send(halves[k], "pipe", 2) for k in back_order}
    mine = call(
        functools.partial(down_pair_kernel, capacity),
        [array(packed_shape, F32)] * expert_total,
        (hidden, vd[0], near_in),
        [VMEM] * 3,
        mib=4,
        flops=2 * rows * col * hidden_width,
        nbytes=piece,
    )
    home = {}
    for k in back_order:
        (done,) = call(
            final_kernel,
            [array(packed_shape)],
            (mine[k], half_in[k]),
            [VMEM, VMEM],
            mib=2,
            nbytes=8 * capacity * col,
        )
        home[k] = send(done, "expert", k) if k else done
    (mixed,) = call(
        functools.partial(mix_kernel, capacity),
        [array((tok_rows, col))],
        (select, scale, *[home[k] for k in range(expert_total)]),
        [VMEM] * (2 + expert_total),
        mib=4,
        flops=4 * rows * tok_rows * col,
        nbytes=2 * rows * col,
    )
    return mixed


def back_order_of(experts):
    return [experts - 1, *range(1, experts - 1), 0]


def solution(mesh):
    experts = mesh.shape["expert"]

    def body(tokens, routes, route_weights, w_gate, w_up, w_down):
        col = tokens.shape[1] // mesh.shape["pipe"]
        fits = (
            mesh.shape["pipe"] == 4
            and experts & (experts - 1) == 0
            and w_gate.shape[0] == 1
            and col % 128 == 0
            and w_gate.shape[2] % 128 == 0
        )
        step = on_device if fits else on_any_mesh
        return step(tokens, routes, route_weights, w_gate, w_up, w_down)

    return jax.shard_map(
        body,
        mesh=mesh,
        in_specs=(
            P(("dp", "expert"), None),
            P(("dp", "expert"), None),
            P(("dp", "expert"), None),
            P("expert", None, "pipe"),
            P("expert", None, "pipe"),
            P("expert", "pipe", None),
        ),
        out_specs=P(("dp", "expert"), "pipe"),
        check_vma=False,
    )
```

```python
import functools

import jax
import jax.numpy as jnp
from jax import lax
from jax.experimental import pallas as pl
from jax.experimental.pallas import tpu as pltpu
from jax.sharding import PartitionSpec as P


F32 = jnp.float32
BF16 = jnp.bfloat16
HBM = pl.BlockSpec(memory_space=pltpu.HBM)
VMEM = pl.BlockSpec(memory_space=pltpu.VMEM)
MIB = 1 << 20
PACK_COST = 0
FETCH = {1: 1}
DOWN_STEP = 256
LOCAL_COST = 12 << 20


def capacity_of(tok_rows, expert_total, replica_count):
    per_expert = (2 * tok_rows + expert_total - 1) // expert_total
    return min(tok_rows, replica_count * (per_expert // replica_count + 1))


def slot_table(route_rows, expert_total):
    choices = route_rows.reshape(-1)
    expert_ids = jnp.arange(expert_total, dtype=jnp.int32)
    matches = (choices[None, :] == expert_ids[:, None]).astype(jnp.int32)
    rank_of = jnp.cumsum(matches, axis=1) - 1
    return (choices, jnp.sum(rank_of * matches, axis=0))


def on_any_mesh(tokens, routes, route_weights, w_gate, w_up, w_down):
    expert_total = w_gate.shape[0] * lax.axis_size("expert")
    pipe_count = lax.axis_size("pipe")
    hidden_width = w_gate.shape[2]
    tok_rows, model_width = tokens.shape
    capacity = capacity_of(tok_rows, expert_total, lax.axis_size("dp"))
    col_share = model_width // pipe_count
    choices, slot_of = slot_table(routes, expert_total)
    target = choices * capacity + slot_of
    column_ids = jnp.arange(expert_total * capacity, dtype=jnp.int32)
    picker = (column_ids[:, None] == target[None, :]).astype(BF16)
    own_columns = lax.dynamic_slice_in_dim(tokens, lax.axis_index("pipe") * col_share, col_share, 1)
    outgoing = jnp.dot(picker, jnp.repeat(own_columns, 2, axis=0), preferred_element_type=F32)
    outgoing = outgoing.astype(BF16).reshape(expert_total, capacity, col_share)
    arrived = lax.all_to_all(outgoing, "expert", split_axis=0, concat_axis=0, tiled=True)
    rows = lax.all_gather(arrived, "pipe", axis=2, tiled=True)
    gate_part = jnp.einsum("gsd,df->gsf", rows, w_gate[0], preferred_element_type=F32)
    up_part = jnp.einsum("gsd,df->gsf", rows, w_up[0], preferred_element_type=F32)
    hidden = (jax.nn.silu(gate_part) * up_part).astype(BF16)
    down_blocks = w_down[0].reshape(hidden_width, pipe_count, col_share)
    block_term = jnp.einsum("gsf,fke->kgse", hidden, down_blocks, preferred_element_type=F32)
    block_term = lax.optimization_barrier(block_term.astype(BF16))
    section = lax.psum_scatter(block_term, "pipe", scatter_dimension=0, tiled=True)
    summed = section.reshape(expert_total, capacity, col_share)
    returned = lax.all_to_all(summed, "expert", split_axis=0, concat_axis=0, tiled=True)
    mixing = (target[:, None] == column_ids[None, :]).astype(F32) * route_weights.reshape(-1)[:, None]
    mixing = mixing.reshape(tok_rows, 2, expert_total * capacity).sum(axis=1)
    mixed = jnp.dot(
        mixing,
        returned.reshape(expert_total * capacity, col_share).astype(F32),
        precision=lax.Precision.HIGHEST,
    )
    return mixed.astype(BF16)


def load_all(pairs, sems):
    copies = [pltpu.make_async_copy(a, b, sems.at[i]) for i, (a, b) in enumerate(pairs)]
    for copy in copies:
        copy.start()
    return copies


def wait_all(copies):
    for copy in copies:
        copy.wait()


def put_packed(out_ref, values, first=0):
    height = values.shape[0]
    for b in range(values.shape[1] // 128):
        at = (first // 128 + b) * height
        out_ref[at : at + height, :] = values[:, b * 128 : (b + 1) * 128]


def take_packed(ref, height, first, count):
    return jnp.concatenate(
        [ref[b * height : (b + 1) * height, :] for b in range(first, first + count)], axis=1
    )


def cols_of(w_ref, share, width):
    lead = (0,) if len(w_ref.shape) == 3 else ()
    return w_ref.at[(*lead, slice(None), pl.ds(pl.multiple_of(share * width, width), width))]


def ranks(routes_t, experts):
    tok_rows = routes_t.shape[1]
    named = (routes_t[0:1, :] == experts) | (routes_t[1:2, :] == experts)
    named = named.astype(F32)
    earlier = lax.broadcasted_iota(jnp.int32, (tok_rows, tok_rows), 0)
    later = lax.broadcasted_iota(jnp.int32, (tok_rows, tok_rows), 1)
    before = (earlier < later).astype(BF16)
    count = jnp.dot(named.astype(BF16), before, preferred_element_type=F32)
    return named, count


def expert_rows(count):
    mine = lax.axis_index("expert")
    return jnp.bitwise_xor(lax.broadcasted_iota(jnp.int32, (count, 1), 0), mine)


def lead_kernel(mark_ref, *refs):
    refs[-1][...] = mark_ref[...]


def pack_kernel(capacity, expert_total, routes_hbm, tokens_hbm, *refs):
    outs = refs[: expert_total - 1]
    mark_ref, routes_ref, own_ref, other_ref, pick_ref, sems = refs[expert_total - 1 :]
    share = lax.axis_index("pipe")
    width = own_ref.shape[1]
    routes_load, own_load, other_load = load_all(
        [
            (routes_hbm, routes_ref),
            (cols_of(tokens_hbm, share, width), own_ref),
            (cols_of(tokens_hbm, jnp.bitwise_xor(share, 2), width), other_ref),
        ],
        sems,
    )
    routes_load.wait()
    named, count = ranks(routes_ref[...], expert_rows(max(8, expert_total)))
    padded = pick_ref.shape[0] // (expert_total - 1)
    slot_ids = lax.broadcasted_iota(jnp.int32, (padded, 1), 0).astype(F32)
    for k in range(1, expert_total):
        chosen = (count[k : k + 1, :] == slot_ids) & (named[k : k + 1, :] > 0.5)
        pick_ref[(k - 1) * padded : k * padded, :] = chosen.astype(BF16)
    own_load.wait()
    picked = jnp.dot(pick_ref[...], own_ref[...], preferred_element_type=F32).astype(BF16)
    for k, out_ref in enumerate(outs):
        put_packed(out_ref, picked[k * padded : k * padded + capacity, :])
    other_load.wait()
    picked = jnp.dot(pick_ref[:padded, :], other_ref[...], preferred_element_type=F32).astype(BF16)
    put_packed(outs[0], picked[:capacity, :], picked.shape[1])
    mark_ref[...] = jnp.zeros_like(mark_ref)


def local_kernel(capacity, expert_total, takes, routes_hbm, weights_hbm, tokens_hbm, down_ref, mark_ref, *refs):
    own_ref, select_ref, scale_ref, *vd_refs, routes_ref, weights_ref, tokens_ref, sems = refs
    small = load_all(
        [(routes_hbm, routes_ref), (weights_hbm, weights_ref), (tokens_hbm, tokens_ref)], sems
    )
    share = lax.axis_index("pipe")
    loads = load_all(
        [
            (cols_of(down_ref, jnp.bitwise_xor(share, take), vd_ref.shape[1]), vd_ref)
            for take, vd_ref in zip(takes, vd_refs)
        ],
        sems.at[pl.ds(len(small), len(takes))],
    )
    wait_all(small)

    @pl.when(share >= 0)
    def _():
        local_work(
            capacity, expert_total, routes_ref, weights_ref, tokens_ref, own_ref, select_ref, scale_ref
        )

    wait_all(loads)


def local_work(
    capacity, expert_total, routes_ref, weights_ref, tokens_ref, own_ref, select_ref, scale_ref
):
    tok_rows = tokens_ref.shape[0]
    routes_t = routes_ref[...]
    experts = expert_rows(max(8, expert_total))
    named, count = ranks(routes_t, experts)
    slot_ids = lax.broadcasted_iota(jnp.int32, (capacity, 1), 0).astype(F32)
    chosen = ((count[0:1, :] == slot_ids) & (named[0:1, :] > 0.5)).astype(BF16)
    own_ref[...] = jnp.dot(chosen, tokens_ref[...], preferred_element_type=F32).astype(BF16)
    line = lax.broadcasted_iota(jnp.int32, (tok_rows, tok_rows), 0)
    lane = lax.broadcasted_iota(jnp.int32, (tok_rows, tok_rows), 1)
    eye = line == lane
    lane_slots = lax.broadcasted_iota(jnp.int32, (1, capacity), 1).astype(F32)

    def column(row):
        return jnp.sum(jnp.where(eye, row, 0.0), axis=1, keepdims=True)

    for c in range(2):
        route = routes_t[c : c + 1, :]
        slot = jnp.sum(jnp.where(route == experts, count, 0.0), axis=0, keepdims=True)
        slot_col = column(slot)
        route_col = column(jnp.bitwise_xor(route, lax.axis_index("expert")).astype(F32))
        scale_ref[c * tok_rows : (c + 1) * tok_rows, :] = jnp.broadcast_to(
            column(weights_ref[c : c + 1, :]), (tok_rows, scale_ref.shape[1])
        )
        for k in range(expert_total):
            hit = (slot_col == lane_slots) & (route_col == float(k))
            select_ref[k, c * tok_rows : (c + 1) * tok_rows, :] = hit.astype(BF16)


def join_kernel(j, capacity, own_ref, *refs):
    parts, out_ref = refs[:-1], refs[-1]
    width = out_ref.shape[1]
    share = jnp.bitwise_xor(lax.axis_index("pipe"), j)
    out_ref[0:capacity, :] = own_ref[:, pl.ds(pl.multiple_of(share * width, width), width)]
    blocks = width // 128
    for i, part in enumerate(parts):
        first = blocks if j and part.shape[0] > blocks * capacity else 0
        out_ref[(i + 1) * capacity : (i + 2) * capacity, :] = take_packed(part, capacity, first, blocks)


def gate_up_kernel(j, take, step, first, last, x_ref, vg_ref, vu_ref, *refs):
    sums_in = () if first else refs[:2]
    refs = refs[len(sums_in) :]
    share = lax.axis_index("pipe")
    loads = []
    if take is not None:
        down_ref, *refs, vd_ref, sems = refs
        source = cols_of(down_ref, jnp.bitwise_xor(share, take), vd_ref.shape[1])
        loads = load_all([(source, vd_ref)], sems)
    outs = refs
    width, height = vg_ref.shape[-1], x_ref.shape[1]
    rows = pl.ds(pl.multiple_of(jnp.bitwise_xor(share, j) * height, height), height)

    @pl.when(share >= 0)
    def _():
        for f in range(0, width, step):
            gate = jnp.dot(x_ref[...], vg_ref[0, rows, f : f + step], preferred_element_type=F32)
            up = jnp.dot(x_ref[...], vu_ref[0, rows, f : f + step], preferred_element_type=F32)
            if not first:
                gate += sums_in[0][:, f : f + step]
                up += sums_in[1][:, f : f + step]
            if last:
                outs[0][:, f : f + step] = (gate / (1.0 + jnp.exp(-gate)) * up).astype(BF16)
            else:
                outs[0][:, f : f + step] = gate
                outs[1][:, f : f + step] = up

    wait_all(loads)


def down_dots(j, hidden_ref, vd_ref, width):
    step = DOWN_STEP if width % DOWN_STEP == 0 else width
    start = jnp.bitwise_xor(lax.axis_index("pipe"), j) * width
    for f in range(0, width, step):
        if len(vd_ref.shape) == 2:
            weights = vd_ref[:, f : f + step]
        else:
            weights = vd_ref[0, :, pl.ds(pl.multiple_of(start + f, 128), step)]
        yield slice(f, f + step), jnp.dot(hidden_ref[...], weights, preferred_element_type=F32)


def down_kernel(picks, hidden_ref, *refs):
    for j, vd_ref, out_ref in zip(picks, refs, refs[len(picks) :]):
        for columns, term in down_dots(j, hidden_ref, vd_ref, out_ref.shape[1]):
            out_ref[:, columns] = term.astype(out_ref.dtype)


def pair_kernel(capacity, mine_ref, other_ref, *outs):
    for k, out_ref in enumerate(outs):
        rows = slice(k * capacity, (k + 1) * capacity)
        total = mine_ref[rows, :] + other_ref[rows, :].astype(F32)
        put_packed(out_ref, total.astype(BF16))


def down_pair_kernel(capacity, hidden_ref, vd_ref, other_ref, *outs):
    for columns, term in down_dots(0, hidden_ref, vd_ref, other_ref.shape[1]):
        total = term + other_ref[:, columns].astype(F32)
        for k, out_ref in enumerate(outs):
            put_packed(out_ref, total[k * capacity : (k + 1) * capacity, :], columns.start)


def final_kernel(mine_ref, other_ref, out_ref):
    out_ref[...] = (mine_ref[...] + other_ref[...].astype(F32)).astype(BF16)


def mix_terms(capacity, picks, select_ref, parts, b):
    total = None
    for k, part in zip(picks, parts):
        rows = part[b * capacity : (b + 1) * capacity, :]
        term = jnp.dot(select_ref[k], rows, preferred_element_type=F32)
        total = term if total is None else total + term
    return total


def premix_kernel(capacity, picks, select_ref, *refs):
    parts, out_ref = refs[:-1], refs[-1]
    for b in range(out_ref.shape[1] // 128):
        out_ref[:, b * 128 : (b + 1) * 128] = mix_terms(capacity, picks, select_ref, parts, b)


def mix_kernel(capacity, picks, select_ref, scale_ref, sums_ref, *refs):
    parts, (out_hbm, out_ref, sems) = refs[:-3], refs[-3:]
    tok_rows = out_ref.shape[0]
    copies = []
    for b in range(out_ref.shape[1] // 128):
        columns = slice(b * 128, (b + 1) * 128)
        total = mix_terms(capacity, picks, select_ref, parts, b) + sums_ref[:, columns]
        weighted = total * scale_ref[...]
        out_ref[:, columns] = (weighted[:tok_rows, :] + weighted[tok_rows:, :]).astype(BF16)
        if b % 2:
            pair = slice((b - 1) * 128, (b + 1) * 128)
            copy = pltpu.make_async_copy(out_ref.at[:, pair], out_hbm.at[:, pair], sems.at[len(copies)])
            copy.start()
            copies.append(copy)
    wait_all(copies)


def call(kernel, outs, args, specs, *, scratch=(), mib, flops=0, nbytes=0, aliases=None, results=VMEM):
    return pl.pallas_call(
        kernel,
        out_shape=outs,
        in_specs=specs,
        out_specs=[results] * len(outs),
        scratch_shapes=scratch,
        input_output_aliases=aliases or {},
        compiler_params=pltpu.CompilerParams(vmem_limit_bytes=int(mib * MIB)),
        cost_estimate=pl.CostEstimate(flops=int(flops), bytes_accessed=int(nbytes), transcendentals=0),
    )(*args)


def on_device(tokens, routes, route_weights, w_gate, w_up, w_down):
    expert_total = lax.axis_size("expert")
    pipe_count = lax.axis_size("pipe")
    hidden_width = w_gate.shape[2]
    tok_rows, model_width = tokens.shape
    capacity = capacity_of(tok_rows, expert_total, lax.axis_size("dp"))
    col = model_width // pipe_count
    rows = expert_total * capacity
    piece = col * hidden_width * 2
    dma = pltpu.SemaphoreType.DMA
    others = range(1, expert_total)

    def send(v, axis, shift):
        return lax.ppermute(v, axis, [(i, i ^ shift) for i in range(lax.axis_size(axis))])

    def array(shape, dtype=BF16):
        return jax.ShapeDtypeStruct(shape, dtype)

    def in_hbm(v):
        return pltpu.with_memory_space_constraint(v, pltpu.HBM)

    packed_shape = (capacity * col // 128, 128)

    tall = pltpu.VMEM((hidden_width, col), BF16)
    routes_t = routes.T
    padded = (capacity + 15) // 16 * 16
    *packed, mark = call(
        functools.partial(pack_kernel, capacity, expert_total),
        [array((2 * packed_shape[0], 128))]
        + [array(packed_shape)] * (expert_total - 2)
        + [array((8, 128), F32)],
        (in_hbm(routes_t), in_hbm(tokens)),
        [HBM, HBM],
        scratch=[
            pltpu.VMEM((2, tok_rows), jnp.int32),
            pltpu.VMEM((tok_rows, col), BF16),
            pltpu.VMEM((tok_rows, col), BF16),
            pltpu.VMEM(((expert_total - 1) * padded, tok_rows), BF16),
            dma((3,)),
        ],
        mib=4,
        flops=2 * rows * tok_rows * col,
        nbytes=PACK_COST,
    )
    (mark,) = call(lead_kernel, [array((8, 128), F32)], (mark, in_hbm(w_gate), in_hbm(w_up)), [VMEM, HBM, HBM], mib=1)
    order = sorted(others, reverse=True)
    arrived = {k: send(packed[k - 1], "expert", k) for k in order}

    takes = (3, 2)
    own_rows, select, scale, *fetched = call(
        functools.partial(local_kernel, capacity, expert_total, takes),
        [
            array((capacity, model_width)),
            array((expert_total, 2 * tok_rows, capacity)),
            array((2 * tok_rows, 128), F32),
            *[tall for _ in takes],
        ],
        (in_hbm(routes_t), in_hbm(route_weights.T), in_hbm(tokens), in_hbm(w_down), mark),
        [HBM, HBM, HBM, HBM, VMEM],
        scratch=[
            pltpu.VMEM((2, tok_rows), jnp.int32),
            pltpu.VMEM((2, tok_rows), F32),
            pltpu.VMEM((tok_rows, model_width), BF16),
            dma((3 + len(takes),)),
        ],
        mib=4,
        flops=2 * rows * tok_rows * model_width,
        nbytes=LOCAL_COST,
    )
    vg = pltpu.with_memory_space_constraint(w_gate, pltpu.VMEM)
    vu = pltpu.with_memory_space_constraint(w_up, pltpu.VMEM)

    def join(j, parts):
        (out,) = call(
            functools.partial(join_kernel, j, capacity),
            [array((rows, col))],
            (own_rows, *[parts[k] for k in others]),
            [VMEM] * expert_total,
            mib=2,
            nbytes=2 * rows * col,
        )
        return out

    crossed = {k: send(arrived[k], "pipe", 2) for k in order if k != 1}
    crossed[1] = arrived[1]
    x0 = join(0, arrived)
    x1 = send(x0, "pipe", 1)
    x2 = join(2, crossed)
    x3 = send(x2, "pipe", 1)

    sums = ()
    vd = {0: pltpu.with_memory_space_constraint(w_down, pltpu.VMEM), **dict(zip(takes, fetched))}
    total = pltpu.VMEM((rows, hidden_width), F32)
    for j, x in enumerate((x0, x1, x2, x3)):
        first, last = j == 0, j == pipe_count - 1
        take = FETCH.get(j)
        fetch = take is not None
        outs = call(
            functools.partial(gate_up_kernel, j, take, min(256, hidden_width), first, last),
            ([pltpu.VMEM((rows, hidden_width), BF16)] if last else [total, total]) + [tall] * fetch,
            (x, vg, vu, *sums) + (in_hbm(w_down),) * fetch,
            [VMEM] * (3 + len(sums)) + [HBM] * fetch,
            scratch=[dma((1,))] * fetch,
            mib=6,
            flops=4 * rows * col * hidden_width,
            nbytes=2 * piece,
            aliases={} if first or last else {3: 0, 4: 1},
        )
        if fetch:
            vd[take] = outs[-1]
        sums = tuple(outs[: 1 if last else 2])
    (hidden,) = sums

    def down(picks, dtypes):
        return call(
            functools.partial(down_kernel, picks),
            [array((rows, col), d) for d in dtypes],
            (hidden, *[vd[j] for j in picks]),
            [VMEM] * (1 + len(picks)),
            mib=4,
            flops=2 * rows * col * hidden_width * len(picks),
            nbytes=piece,
        )

    (far_other,) = down((3,), (BF16,))
    far_in = send(far_other, "pipe", 1)
    far_mine, near_other = down((2, 1), (F32, BF16))
    near_in = send(near_other, "pipe", 1)
    halves = call(
        functools.partial(pair_kernel, capacity),
        [array(packed_shape)] * expert_total,
        (far_mine, far_in),
        [VMEM, VMEM],
        mib=4,
        nbytes=8 * rows * col,
    )
    back_order = back_order_of(expert_total)
    half_in = {k: send(halves[k], "pipe", 2) for k in back_order}
    mine = call(
        functools.partial(down_pair_kernel, capacity),
        [array(packed_shape, F32)] * expert_total,
        (hidden, vd[0], near_in),
        [VMEM] * 3,
        mib=4,
        flops=2 * rows * col * hidden_width,
        nbytes=piece,
    )
    home = {}
    for k in back_order:
        (done,) = call(
            final_kernel, [array(packed_shape)], (mine[k], half_in[k]), [VMEM, VMEM], mib=2, nbytes=8 * capacity * col
        )
        home[k] = send(done, "expert", k) if k else done
    last = back_order[-2:-1]
    early = [k for k in range(expert_total) if k not in last]
    (premixed,) = call(
        functools.partial(premix_kernel, capacity, early),
        [array((2 * tok_rows, col), F32)],
        (select, *[home[k] for k in early]),
        [VMEM] * (1 + len(early)),
        mib=4,
        flops=4 * rows * tok_rows * col,
    )
    (mixed,) = call(
        functools.partial(mix_kernel, capacity, last),
        [array((tok_rows, col))],
        (select, scale, premixed, *[home[k] for k in last]),
        [VMEM] * (3 + len(last)),
        scratch=[pltpu.VMEM((tok_rows, col), BF16), dma((col // 256,))],
        mib=4,
        flops=4 * capacity * tok_rows * col,
        results=HBM,
    )
    return mixed


def back_order_of(experts):
    return [experts - 1, *range(1, experts - 1), 0]


def solution(mesh):
    experts = mesh.shape["expert"]

    def body(tokens, routes, route_weights, w_gate, w_up, w_down):
        col = tokens.shape[1] // mesh.shape["pipe"]
        fits = (
            mesh.shape["pipe"] == 4
            and experts > 2
            and experts & (experts - 1) == 0
            and w_gate.shape[0] == 1
            and col % 128 == 0
            and w_gate.shape[2] % 128 == 0
        )
        step = on_device if fits else on_any_mesh
        return step(tokens, routes, route_weights, w_gate, w_up, w_down)

    return jax.shard_map(
        body,
        mesh=mesh,
        in_specs=(
            P(("dp", "expert"), None),
            P(("dp", "expert"), None),
            P(("dp", "expert"), None),
            P("expert", None, "pipe"),
            P("expert", None, "pipe"),
            P("expert", "pipe", None),
        ),
        out_specs=P(("dp", "expert"), "pipe"),
        check_vma=False,
    )
```
